256 devices in a mesh: dp: 8 (over x, z_hi), context: 32 (over y, z_lo, core).
Axes of the slice: x: 4, y: 4, z: 8 (z_hi: 2, z_lo: 4; z = z_hi * 4 + z_lo), core: 2. Of those that a mesh axis runs over, the one named last changes fastest.
Arguments:
- grad_out: bfloat16 [8, 4096, 4096], P('dp', 'context'), may hold values from -6 to 6
- attn: bfloat16 [8, 4096, 4096], P('dp', 'context'), may hold values from -0.032958984 to 0.032958984
- w_out: bfloat16 [4096, 4096], P('context'), may hold values from -0.09375 to 0.09375
Outputs:
- grad_attn: bfloat16 [8, 4096, 4096], P('dp', None, 'context')
- grad_w: bfloat16 [4096, 4096], P('context')
The draws below stay inside these ranges and needn't reach their ends.
All inputs are finite; a program needn't handle non-finite values.
Results may differ from the reference program's by a relative error of at most 0.013.
Values may be sent and summed in bfloat16 or wider, within the bound.
No kernel may reach another device: no remote copies, remote signals or barrier semaphores. Data moves between devices by JAX's collectives and lax.ppermute only.
A program may use at most 128 MiB of HBM per device.

```python
import jax
import jax.numpy as jnp
from jax import lax

D = 4096
HD = 4096
LEN = 4096
SEQS = 8


def shard_levels(key, shape, split, smallest, top_value):
    loudness, own = 1.0, jax.random.fold_in(key, 6)
    for dim, parts in split:
        heights = jnp.exp(jax.random.uniform(jax.random.fold_in(own, dim), (parts,), jnp.float32, smallest / len(split), top_value / len(split)))
        loudness = loudness * jnp.repeat(heights, shape[dim] // parts).reshape([-1 if axis == dim else 1 for axis in range(len(shape))])
    return loudness


def scatter_about(stream_key, shape, width, reach, split=(), kind=jnp.bfloat16):
    entries = width * jax.random.normal(stream_key, shape, jnp.float32)
    if split:
        entries = entries * shard_levels(stream_key, shape, split, -0.22, 0.18)
    return jnp.clip(entries, -reach, reach).astype(kind)


def setup_inputs(seed: int = 0) -> dict:
    seeds = jax.random.split(jax.random.key(seed), 4)
    grad_out = scatter_about(seeds[0], (SEQS, LEN, D), 1.0, 6.0, ((0, 8), (1, 32)))
    attn = scatter_about(seeds[1], (SEQS, LEN, HD), ((SEQS * LEN) ** -0.5), 0.032958984, ((0, 8), (1, 32)))
    w_out = scatter_about(seeds[2], (HD, D), HD ** -0.5, 0.09375, ((0, 32),))
    return {"grad_out": grad_out, "attn": attn, "w_out": w_out}


def reference(grad_out, attn, w_out):
    def one_sequence(totals, inputs):
        cotangent, activations = inputs
        head_grad = jnp.dot(cotangent, w_out.T, preferred_element_type=jnp.float32).astype(jnp.bfloat16)
        partial_grad = jnp.dot(activations.T, cotangent, preferred_element_type=jnp.float32).astype(jnp.bfloat16)
        partial_grad = lax.optimization_barrier(partial_grad)
        return totals + partial_grad.astype(jnp.float32), head_grad

    start_totals = jnp.zeros((w_out.shape[0], w_out.shape[1]), jnp.float32)
    totals, head_grads = lax.scan(one_sequence, start_totals, (grad_out, attn))
    return head_grads, totals.astype(jnp.bfloat16)
```

```python
import jax
import jax.numpy as jnp
from jax import lax
from jax.sharding import Mesh, PartitionSpec as P

CHUNKS = 2
RING8 = ("h", "l")


def shift(v, axis, by):
    n = lax.axis_size(axis)
    return lax.ppermute(v, axis, [(i, (i + by) % n) for i in range(n)])


def pick(v, index, axis):
    return lax.dynamic_index_in_dim(v, index, axis, keepdims=False)


def around(own, axis):
    half = own.shape[0] // 2
    above = shift(own, axis, -1)
    below = shift(own, axis, 1)
    far_a = shift(above[:half], axis, -1)
    far_b = shift(below[half:], axis, 1)
    return [own, above, jnp.concatenate([far_a, far_b], 0), below]


def rolled(pieces, by):
    twice = jnp.stack(pieces + pieces)
    n = len(pieces)
    return lax.dynamic_slice_in_dim(twice, (n - by) & (n - 1), n, 0)


def local(grad_out, attn, w_out):
    f32, bf16 = jnp.float32, jnp.bfloat16
    g = grad_out[0]
    a = attn[0]
    toks, feats = g.shape
    heads = w_out.shape[0]
    x, y, l, c = (lax.axis_index(n) for n in ("x", "y", "l", "c"))

    a = a.reshape(toks, 4, 4, 2, heads)
    a_own = pick(a, c, 3)
    a_sib = shift(pick(a, 1 - c, 3), "c", 1)
    a2 = jnp.stack([a_own, a_sib])
    a_pieces = [pick(a2, y, 2)]
    for d in (1, 2, 3):
        a_pieces.append(shift(pick(a2, (y - d) & 3, 2), "y", -d))
    acts = jnp.stack(a_pieces, 1).reshape(2 * 4 * toks, 4 * heads)

    w = jnp.concatenate(around(w_out, RING8), 0)

    step = feats // CHUNKS
    quarter = heads // 4
    g_cols, w_rows = [], []
    for j in range(CHUNKS):
        ring = around(g[:, j * step:(j + 1) * step], "y")
        sib = [shift(p, "c", 1) for p in ring]
        gj = jnp.concatenate(ring + sib, 0)
        g_cols.append(gj)
        part = lax.dot_general(acts, gj, (((0,), (0,)), ((), ())), preferred_element_type=f32).astype(bf16)
        part = part.reshape(4, 4, quarter, step)
        tot = pick(part, x, 1).astype(f32)
        for d in (1, 2, 3):
            tot = tot + shift(pick(part, (x + d) & 3, 1), "x", d).astype(f32)
        tot = tot.astype(bf16)
        h2 = quarter // 2
        far = pick(tot, (l + 2) & 3, 0)
        acc = pick(tot, l, 0).astype(f32)
        acc = acc + shift(pick(tot, (l + 1) & 3, 0), RING8, 1).astype(f32)
        acc = acc + shift(pick(tot, (l + 3) & 3, 0), RING8, -1).astype(f32)
        acc = acc + jnp.concatenate([shift(far[:h2], RING8, -2), shift(far[h2:], RING8, 2)], 0).astype(f32)
        acc = acc.astype(bf16)
        done = (acc.astype(f32) + shift(acc, "h", 1).astype(f32)).astype(bf16)
        rows = [done] + [shift(done, "x", -d) for d in (1, 2, 3)]
        w_rows.append(rolled(rows, x).reshape(heads, step))
    grad_w = jnp.concatenate(w_rows, 1)

    gall = jnp.concatenate(g_cols, 1)
    res = lax.dot_general(gall, w, (((1,), (1,)), ((), ())), preferred_element_type=f32).astype(bf16)
    res = res.reshape(2, 4, toks, 4, heads)
    outs = [res[:, :, :, 0]] + [shift(res[:, :, :, 4 - d], "l", -d) for d in (1, 2, 3)]
    out = rolled(outs, l)
    out = jnp.where(c == 0, out, out[:, ::-1])
    out = jnp.concatenate([out, out], 2)
    out = lax.dynamic_slice_in_dim(out, (4 - y) & 3, 4, 2)
    out = out.transpose(2, 0, 1, 3, 4).reshape(1, 4 * 4 * 2 * toks, heads)
    return out, grad_w


def solution(mesh):
    fine = Mesh(mesh.devices.reshape(4, 2, 4, 4, 2), ("x", "h", "y", "l", "c"))
    dp, context = ("x", "h"), ("y", "l", "c")
    in_specs = (P(dp, context, None), P(dp, context, None), P(context, None))
    out_specs = (P(dp, None, context), P(context, None))
    return jax.shard_map(local, mesh=fine, in_specs=in_specs, out_specs=out_specs, check_vma=False)
```

```python
import jax
import jax.numpy as jnp
from jax import lax
from jax.sharding import Mesh, PartitionSpec as P

CHUNKS = (2048, 2048)
RING8 = ("h", "l")


def shift(v, axis, by):
    n = lax.axis_size(axis)
    return lax.ppermute(v, axis, [(i, (i + by) % n) for i in range(n)])


def pick(v, index, axis):
    return lax.dynamic_index_in_dim(v, index, axis, keepdims=False)


def around(own, axis):
    half = own.shape[0] // 2
    above = shift(own, axis, -1)
    below = shift(own, axis, 1)
    far_a = shift(above[:half], axis, -1)
    far_b = shift(below[half:], axis, 1)
    return [own, above, far_a, far_b, below]


def rolled(pieces, by):
    n = len(pieces)
    twice = jnp.stack(pieces + pieces)
    return lax.dynamic_slice_in_dim(twice, (n - by) & (n - 1), n, 0)


def local(grad_out, attn, w_out):
    f32, bf16 = jnp.float32, jnp.bfloat16
    g = grad_out[0]
    a = attn[0]
    toks, feats = g.shape
    heads = w_out.shape[0]
    quarter = heads // 4
    x, l = lax.axis_index("x"), lax.axis_index("l")

    cuts, at = [], 0
    for size in CHUNKS:
        size = size * feats // sum(CHUNKS)
        cuts.append((at, at + size))
        at += size
    g_cols = [lax.all_gather(g[:, lo:hi], ("y", "c"), axis=0, tiled=True) for lo, hi in cuts]

    w = jnp.concatenate(around(w_out, RING8), 0)

    a = a.reshape(toks, 4, 4, 2, heads).transpose(1, 3, 0, 2, 4).reshape(8, toks, 4 * heads)
    acts = lax.all_to_all(a, ("y", "c"), split_axis=0, concat_axis=0, tiled=True).reshape(8 * toks, 4 * heads)

    sums = []
    for j, gj in enumerate(g_cols):
        part = lax.dot_general(acts, gj, (((0,), (0,)), ((), ())), preferred_element_type=f32).astype(bf16)
        part = part.reshape(4, 4, quarter, -1)
        tot = pick(part, x, 1).astype(f32)
        for d in (1, 2, 3):
            tot = tot + shift(pick(part, (x + d) & 3, 1), "x", d).astype(f32)
        tot = tot.astype(bf16)
        acc = pick(tot, l, 0).astype(f32)
        acc = acc + shift(pick(tot, (l + 1) & 3, 0), RING8, 1).astype(f32)
        acc = acc + shift(pick(tot, (l + 3) & 3, 0), RING8, -1).astype(f32)
        acc = acc + shift(pick(tot, (l + 2) & 3, 0), RING8, 2 if j % 2 else -2).astype(f32)
        acc = acc.astype(bf16)
        sums.append((acc.astype(f32) + shift(acc, "h", 1).astype(f32)).astype(bf16))
    done = jnp.concatenate(sums, 1)
    grad_w = rolled([done] + [shift(done, "x", -d) for d in (1, 2, 3)], x).reshape(heads, feats)

    gall = jnp.concatenate(g_cols, 1)
    res = lax.dot_general(gall, w, (((1,), (1,)), ((), ())), preferred_element_type=f32).astype(bf16)
    res = res.reshape(4, 2, toks, 4, heads)
    outs = [res[:, :, :, 0]] + [shift(res[:, :, :, 4 - d], "l", -d) for d in (1, 2, 3)]
    out = rolled(outs, l)
    out = out.transpose(1, 0, 2, 3, 4).reshape(1, 4 * 4 * 2 * toks, heads)
    return out, grad_w


def solution(mesh):
    fine = Mesh(mesh.devices.reshape(4, 2, 4, 4, 2), ("x", "h", "y", "l", "c"))
    dp, context = ("x", "h"), ("y", "l", "c")
    in_specs = (P(dp, context, None), P(dp, context, None), P(context, None))
    out_specs = (P(dp, None, context), P(context, None))
    return jax.shard_map(local, mesh=fine, in_specs=in_specs, out_specs=out_specs, check_vma=False)
```

```python
import jax
import jax.numpy as jnp
from jax import lax
from jax.sharding import Mesh, PartitionSpec as P

CHUNKS = (2048, 2048)
RING8 = ("h", "l")


def shift(v, axis, by):
    n = lax.axis_size(axis)
    return lax.ppermute(v, axis, [(i, (i + by) % n) for i in range(n)])


def exchange(v, axis):
    return lax.all_to_all(v, axis, split_axis=0, concat_axis=0, tiled=True)


def after(v, *others):
    return lax.optimization_barrier((v, *others))[0]


def around(own, axis):
    half = own.shape[0] // 2
    above = shift(own, axis, -1)
    below = shift(own, axis, 1)
    far_a = shift(above[:half], axis, -1)
    far_b = shift(below[half:], axis, 1)
    return [own, above, far_a, far_b, below]


def local(grad_out, attn, w_out):
    f32, bf16 = jnp.float32, jnp.bfloat16
    g = grad_out[0]
    a = attn[0]
    toks, feats = g.shape
    heads = w_out.shape[0]
    quarter = heads // 4
    l = lax.axis_index("l")

    cuts, at = [], 0
    for size in CHUNKS:
        size = size * feats // sum(CHUNKS)
        cuts.append((at, at + size))
        at += size
    g_cols = [lax.all_gather(g[:, lo:hi], ("y", "c"), axis=0, tiled=True) for lo, hi in cuts]

    a = a.reshape(toks, 4, 4, 2, heads).transpose(1, 3, 0, 2, 4).reshape(8, toks, 4 * heads)
    acts = exchange(a, ("y", "c")).reshape(8 * toks, 4 * heads)

    w_parts = around(w_out, RING8)

    sums, part = [], None
    for gj in g_cols:
        if part is not None:
            gj = after(gj, part)
        part = lax.dot_general(acts, gj, (((0,), (0,)), ((), ())), preferred_element_type=f32).astype(bf16)
        part = part.reshape(4, 4, quarter, -1)
        tot = exchange(part.transpose(1, 0, 2, 3), "x").astype(f32).sum(0).astype(bf16)
        tot = exchange(tot, "l").astype(f32).sum(0).astype(bf16)
        tot = (tot.astype(f32) + shift(tot, "h", 1).astype(f32)).astype(bf16)
        sums.append(exchange(jnp.broadcast_to(tot[None], (4,) + tot.shape), "x").reshape(heads, -1))
    grad_w = jnp.concatenate(sums, 1)

    w = jnp.concatenate(w_parts, 0)
    w = lax.dynamic_slice_in_dim(jnp.concatenate([w, w], 0), ((4 - l) & 3) * heads, 4 * heads, 0)
    gall = after(jnp.concatenate(g_cols, 1), part)
    res = lax.dot_general(gall, w, (((1,), (1,)), ((), ())), preferred_element_type=f32).astype(bf16)
    res = res.reshape(8 * toks, 4, heads).transpose(1, 0, 2)
    out = exchange(res, "l")
    out = out.reshape(4, 4, 2 * toks, heads).transpose(1, 0, 2, 3).reshape(1, 4 * 8 * toks, heads)
    return out, grad_w


def solution(mesh):
    fine = Mesh(mesh.devices.reshape(4, 2, 4, 4, 2), ("x", "h", "y", "l", "c"))
    dp, context = ("x", "h"), ("y", "l", "c")
    in_specs = (P(dp, context, None), P(dp, context, None), P(context, None))
    out_specs = (P(dp, None, context), P(context, None))
    return jax.shard_map(local, mesh=fine, in_specs=in_specs, out_specs=out_specs, check_vma=False)
```

```python
import jax
import jax.numpy as jnp
from jax import lax
from jax.experimental import pallas as pl
from jax.experimental.pallas import tpu as pltpu
from jax.sharding import Mesh, PartitionSpec as P

CHUNKS = (2048, 2048)
RING8 = ("h", "l")
F32, BF16 = jnp.float32, jnp.bfloat16


def shift(v, axis, by):
    n = lax.axis_size(axis)
    return lax.ppermute(v, axis, [(i, (i + by) % n) for i in range(n)])


def exchange(v, axis):
    return lax.all_to_all(v, axis, split_axis=0, concat_axis=0, tiled=True)


def after(v, *others):
    return lax.optimization_barrier((v, *others))[0]


def pick(v, index):
    return lax.dynamic_index_in_dim(v, index, 0, keepdims=False)


def gathered(acc):
    return exchange(jnp.broadcast_to(acc[None], (4,) + acc.shape), "x")


def partial_kernel(at, acts, own, sib, *refs):
    outs, total_ref = refs[:-1], refs[-1]
    x, c = at[0], at[2]
    blocks, rows, _ = outs[0].shape
    total = 0.0
    for which, tokens in ((c, own), (1 - c, sib)):
        lhs = jnp.concatenate([acts[i, which] for i in range(acts.shape[0])], axis=1)
        total = total + jnp.dot(lhs, tokens[...], preferred_element_type=F32)
    total_ref[...] = total.reshape(total_ref.shape)
    for r, out in enumerate(outs):
        out[...] = total_ref[:, (x + r) & 3].astype(out.dtype)


def partial(at, acts, own, sib):
    y, _, heads, toks = acts.shape
    cols = own.shape[1]
    wide = min(512, cols)
    rows = heads // 16
    return pl.pallas_call(
        partial_kernel,
        grid_spec=pltpu.PrefetchScalarGridSpec(
            num_scalar_prefetch=1,
            grid=(cols // wide,),
            in_specs=[
                pl.BlockSpec(acts.shape, lambda i, at: (0, 0, 0, 0)),
                pl.BlockSpec((y * toks, wide), lambda i, at: (0, i)),
                pl.BlockSpec((y * toks, wide), lambda i, at: (0, i)),
            ],
            out_specs=[pl.BlockSpec((4, rows, wide), lambda i, at: (0, 0, i))] * 4,
            scratch_shapes=[pltpu.VMEM((4, 4, rows, wide), F32)],
        ),
        out_shape=[jax.ShapeDtypeStruct((4, rows, cols), BF16)] * 4,
        cost_estimate=pl.CostEstimate(
            flops=4 * heads * y * toks * cols, transcendentals=0,
            bytes_accessed=4 * y * toks * cols + 2 * heads * cols + 2 * acts.size),
        name="partial_grad_w",
    )(at, acts, own, sib)


def inputs_kernel(chunks, at, *refs):
    owns, sibs = refs[:chunks], refs[chunks:2 * chunks]
    w0, w1, w2a, w2b, w3, out = refs[2 * chunks:]
    l, c = at[1], at[2]
    heads = w0.shape[0]
    weights = jnp.concatenate([w0[...], w1[...], w2a[...], w2b[...], w3[...]], axis=0)
    for which, tokens in ((c, owns), (1 - c, sibs)):
        total, lo = 0.0, 0
        for ref in tokens:
            hi = lo + ref.shape[1]
            total = total + lax.dot_general(
                ref[...], weights[:, lo:hi], (((1,), (1,)), ((), ())), preferred_element_type=F32)
            lo = hi
        total = total.astype(out.dtype).reshape(out.shape[1], out.shape[3], 4, heads)
        for d in range(4):
            out[(l + d) & 3, :, which] = total[:, :, d]


def inputs_grad(at, owns, sibs, w_parts):
    heads, feats = w_parts[0].shape
    toks = owns[0].shape[0] // 4
    steps = 2
    tall = owns[0].shape[0] // steps
    whole = lambda w: pl.BlockSpec(w.shape, lambda i, at: (0, 0))
    rows = [pl.BlockSpec((tall, o.shape[1]), lambda i, at: (i, 0)) for o in owns]
    return pl.pallas_call(
        lambda at, *refs: inputs_kernel(len(owns), at, *refs),
        grid_spec=pltpu.PrefetchScalarGridSpec(
            num_scalar_prefetch=1,
            grid=(steps,),
            in_specs=rows + rows + [whole(w) for w in w_parts],
            out_specs=pl.BlockSpec((4, 4 // steps, 2, toks, heads), lambda i, at: (0, i, 0, 0, 0)),
        ),
        out_shape=jax.ShapeDtypeStruct((4, 4, 2, toks, heads), BF16),
        cost_estimate=pl.CostEstimate(
            flops=2 * 8 * toks * feats * 4 * heads, transcendentals=0,
            bytes_accessed=2 * (8 * toks * feats + 4 * heads * feats + 32 * toks * heads)),
        name="grad_attn",
    )(at, *owns, *sibs, *w_parts)


def local(grad_out, attn, w_out):
    g = grad_out[0]
    a = attn[0]
    toks, feats = g.shape
    heads = w_out.shape[0]
    at = jnp.stack([lax.axis_index(n) for n in ("x", "l", "c")]).astype(jnp.int32)

    cuts, lo = [], 0
    for size in CHUNKS:
        size = size * feats // sum(CHUNKS)
        cuts.append((lo, lo + size))
        lo += size
    owns = [lax.all_gather(g[:, lo:hi], "y", axis=0, tiled=True) for lo, hi in cuts]

    a = a.reshape(toks, 4, 4, 2, heads).transpose(1, 3, 2, 4, 0).reshape(8, 4 * heads, toks)
    acts = exchange(a, ("y", "c")).reshape(4, 2, 4 * heads, toks)

    above, below = shift(w_out, RING8, -1), shift(w_out, RING8, 1)

    l = lax.axis_index("l")
    owns[0] = after(owns[0], acts, above, below)
    sums, sibs, part, far = [], [], None, None
    for j, own in enumerate(owns):
        if part is not None:
            owns[j] = own = after(own, *moved, *far)
        sib = shift(own, "c", 1)
        sibs.append(sib)
        part = partial(at, acts, own, sib)
        if j == 0:
            half = heads // 2
            far = [shift(after(above[:half], part[0]), RING8, -1), shift(after(below[half:], part[0]), RING8, 1)]
        moved = [shift(part[d], "x", d) for d in (1, 3, 2)]
        tot = part[0].astype(F32)
        for other in moved:
            tot = tot + other.astype(F32)
        tot = tot.astype(BF16)
        acc = pick(tot, l).astype(F32)
        for d in (1, -1, -2 if j % 2 else 2):
            acc = acc + shift(pick(tot, (l + d) & 3), RING8, d).astype(F32)
        acc = acc.astype(BF16)
        sums.append((acc.astype(F32) + shift(acc, "h", 1).astype(F32)).astype(BF16))
    grad_w = jnp.concatenate([gathered(acc).reshape(heads, -1) for acc in sums], 1)

    owns[0] = after(owns[0], part[0])
    res = inputs_grad(at, owns, sibs, [w_out, above, *far, below])
    pieces = [pick(res, l)] + [shift(pick(res, (l + d) & 3), "l", d) for d in (1, 2, 3)]
    out = jnp.zeros((4, 4, 2, toks, heads), BF16)
    for d, piece in enumerate(pieces):
        out = lax.dynamic_update_slice_in_dim(out, piece[:, None], (l - d) & 3, 1)
    out = out.reshape(1, 4 * 8 * toks, heads)
    return out, grad_w


def solution(mesh):
    fine = Mesh(mesh.devices.reshape(4, 2, 4, 4, 2), ("x", "h", "y", "l", "c"))
    dp, context = ("x", "h"), ("y", "l", "c")
    in_specs = (P(dp, context, None), P(dp, context, None), P(context, None))
    out_specs = (P(dp, None, context), P(context, None))
    return jax.shard_map(local, mesh=fine, in_specs=in_specs, out_specs=out_specs, check_vma=False)
```

```python
import jax
import jax.numpy as jnp
from jax import lax
from jax.experimental import pallas as pl
from jax.experimental.pallas import tpu as pltpu
from jax.sharding import Mesh, PartitionSpec as P

CHUNKS = (5, 3)
RING8 = ("h", "l")
F32, BF16 = jnp.float32, jnp.bfloat16


def shift(v, axis, by):
    n = lax.axis_size(axis)
    return lax.ppermute(v, axis, [(i, (i + by) % n) for i in range(n)])


def exchange(v, axis):
    return lax.all_to_all(v, axis, split_axis=0, concat_axis=0, tiled=True)


def after(v, *others):
    return lax.optimization_barrier((v, *others))[0]


def pick(v, index):
    return lax.dynamic_index_in_dim(v, index, 0, keepdims=False)


def partial_kernel(at, acts, *refs):
    pieces, out, lhs = refs[:10], refs[10], refs[11]
    y, c = at[1], at[3]

    @pl.when(pl.program_id(0) == 0)
    def _():
        toks = acts.shape[3]
        for e in range(2):
            for d in range(4):
                k = 4 * e + d
                lhs[:, k * toks:(k + 1) * toks] = acts[(y + d) & 3, (c + e) & 1]

    rhs = jnp.concatenate([p[...] for p in pieces], axis=0)
    total = jnp.dot(lhs[...], rhs, preferred_element_type=F32).astype(out.dtype)
    parts, blocks, rows, _ = out.shape
    for b in range(blocks):
        for q in range(parts):
            r = (b * parts + q) * rows
            out[q, b] = total[r:r + rows]


def partial(at, acts, pieces, lo, hi):
    y, _, heads, toks = acts.shape
    wide = pieces[0].shape[1] // 8
    rows = heads // 16
    return pl.pallas_call(
        partial_kernel,
        grid_spec=pltpu.PrefetchScalarGridSpec(
            num_scalar_prefetch=1,
            grid=((hi - lo) // wide,),
            in_specs=[pl.BlockSpec(acts.shape, lambda i, at: (0, 0, 0, 0))]
            + [pl.BlockSpec((p.shape[0], wide), lambda i, at: (0, i + lo // wide)) for p in pieces],
            out_specs=pl.BlockSpec((4, 4, rows, wide), lambda i, at: (0, 0, 0, i)),
            scratch_shapes=[pltpu.VMEM((heads, 8 * toks), BF16)],
        ),
        out_shape=jax.ShapeDtypeStruct((4, 4, rows, hi - lo), BF16),
        cost_estimate=pl.CostEstimate(
            flops=2 * heads * 8 * toks * (hi - lo), transcendentals=0,
            bytes_accessed=16 * toks * (hi - lo) + 2 * heads * (hi - lo) + 2 * acts.size),
        name="partial_grad_w",
    )(at, acts, *pieces)


def inputs_kernel(at, *refs):
    pieces, weights, out, acc = refs[:10], refs[10:14], refs[14], refs[15]
    y, l, c = at[1], at[2], at[3]
    k = pl.program_id(0)
    lhs = jnp.concatenate([p[...] for p in pieces], axis=0)
    rhs = jnp.concatenate([w[...] for w in weights], axis=0)
    prod = lax.dot_general(lhs, rhs, (((1,), (1,)), ((), ())), preferred_element_type=F32)

    @pl.when(k == 0)
    def _():
        acc[...] = prod

    @pl.when(k > 0)
    def _():
        acc[...] += prod

    @pl.when(k == pl.num_programs(0) - 1)
    def _():
        toks, heads = out.shape[3:]
        for e in range(2):
            for d in range(4):
                t = (4 * e + d) * toks
                for r in range(4):
                    out[(l + r) & 3, (y + d) & 3, (c + e) & 1] = acc[
                        t:t + toks, r * heads:(r + 1) * heads].astype(out.dtype)


def inputs_grad(at, pieces, weights):
    heads, feats = weights[0].shape
    toks = pieces[0].shape[0]
    deep = feats // 4
    return pl.pallas_call(
        inputs_kernel,
        grid_spec=pltpu.PrefetchScalarGridSpec(
            num_scalar_prefetch=1,
            grid=(4,),
            in_specs=[pl.BlockSpec((p.shape[0], deep), lambda k, at: (0, k)) for p in (*pieces, *weights)],
            out_specs=pl.BlockSpec((4, 4, 2, toks, heads), lambda k, at: (0, 0, 0, 0, 0)),
            scratch_shapes=[pltpu.VMEM((8 * toks, 4 * heads), F32)],
        ),
        out_shape=jax.ShapeDtypeStruct((4, 4, 2, toks, heads), BF16),
        cost_estimate=pl.CostEstimate(
            flops=2 * 8 * toks * feats * 4 * heads, transcendentals=0,
            bytes_accessed=2 * (8 * toks * feats + 4 * heads * feats + 32 * toks * heads)),
        name="grad_attn",
    )(at, *pieces, *weights)


def local(grad_out, attn, w_out):
    g = grad_out[0]
    a = attn[0]
    toks, feats = g.shape
    heads = w_out.shape[0]
    at = jnp.stack([lax.axis_index(n) for n in ("x", "y", "l", "c")]).astype(jnp.int32)
    l = at[2]

    cuts, lo = [], 0
    for size in CHUNKS:
        size = size * feats // sum(CHUNKS)
        cuts.append((lo, lo + size))
        lo += size

    a = a.reshape(toks, 4, 4, 2, heads).transpose(1, 3, 2, 4, 0).reshape(8, 4 * heads, toks)
    acts = exchange(a, ("y", "c")).reshape(4, 2, 4 * heads, toks)

    w_above, w_below = shift(w_out, RING8, -1), shift(w_out, RING8, 1)
    w_far = shift(w_below, RING8, 1)
    weights = [w_out, w_above, w_far, w_below]

    half = toks // 2
    above, below = shift(g, "y", -1), shift(g, "y", 1)
    pieces = [g, above, shift(after(above[:half], acts), "y", -1), shift(after(below[half:], acts), "y", 1), below]
    pieces += [shift(p, "c", 1) for p in pieces]

    x = at[0]
    first = [after(g, *weights[1:])] + pieces[1:]
    tots = []
    for lo, hi in cuts:
        part = partial(at, acts, first, lo, hi)
        first = [after(g, part)] + pieces[1:]
        tots.append(exchange(part, "x").astype(F32).sum(0).astype(BF16))

    res = inputs_grad(at, first, weights)
    back = [pick(res, l)] + [shift(pick(res, (l + d) & 3), "l", d) for d in (1, 2, 3)]

    grad_w = jnp.zeros((4, heads // 4, feats), BF16)
    for j, ((lo, hi), tot) in enumerate(zip(cuts, tots)):
        acc = pick(tot, l).astype(F32)
        for d in (1, -1, -2 if j % 2 else 2):
            acc = acc + shift(pick(tot, (l + d) & 3), RING8, d).astype(F32)
        acc = acc.astype(BF16)
        acc = (acc.astype(F32) + shift(acc, "h", 1).astype(F32)).astype(BF16)
        for d in range(4):
            grad_w = lax.dynamic_update_slice(
                grad_w, (shift(acc, "x", d) if d else acc)[None], ((x - d) & 3, 0, lo))
    grad_w = grad_w.reshape(heads, feats)

    out = jnp.zeros((4, 4, 2, toks, heads), BF16)
    for d, piece in enumerate(back):
        out = lax.dynamic_update_slice_in_dim(out, piece[:, None], (l - d) & 3, 1)
    out = out.reshape(1, 4 * 8 * toks, heads)
    return out, grad_w


def solution(mesh):
    fine = Mesh(mesh.devices.reshape(4, 2, 4, 4, 2), ("x", "h", "y", "l", "c"))
    dp, context = ("x", "h"), ("y", "l", "c")
    in_specs = (P(dp, context, None), P(dp, context, None), P(context, None))
    out_specs = (P(dp, None, context), P(context, None))
    return jax.shard_map(local, mesh=fine, in_specs=in_specs, out_specs=out_specs, check_vma=False)
```

```python
import jax
import jax.numpy as jnp
from jax import lax
from jax.experimental import pallas as pl
from jax.experimental.pallas import tpu as pltpu
from jax.sharding import Mesh, PartitionSpec as P

SPLIT = 4
RING8 = ("h", "l")
F32, BF16 = jnp.float32, jnp.bfloat16


def shift(v, axis, by):
    n = lax.axis_size(axis)
    return lax.ppermute(v, axis, [(i, (i + by) % n) for i in range(n)])


def exchange(v, axis):
    return lax.all_to_all(v, axis, split_axis=0, concat_axis=0, tiled=True)


def after(v, *others):
    return lax.optimization_barrier((v, *others))[0]


def pick(v, index):
    return lax.dynamic_index_in_dim(v, index, 0, keepdims=False)


def partial_kernel(at, acts, *refs):
    pieces, out, lhs = refs[:-2], refs[-2], refs[-1]
    y, c = (at[1], at[3]) if len(pieces) > 1 else (0, 0)

    @pl.when(pl.program_id(0) == 0)
    def _():
        toks = acts.shape[3]
        for d in range(4):
            for e in range(2):
                k = 4 * e + d if len(pieces) > 1 else 2 * d + e
                lhs[:, k * toks:(k + 1) * toks] = acts[(y + d) & 3, (c + e) & 1]

    rhs = jnp.concatenate([p[...] for p in pieces], axis=0)
    total = jnp.dot(lhs[...], rhs, preferred_element_type=F32).astype(out.dtype)
    parts, blocks, rows, _ = out.shape
    for b in range(blocks):
        for q in range(parts):
            r = (b * parts + q) * rows
            out[q, b] = total[r:r + rows]


def partial(at, acts, pieces, lo, hi):
    y, _, heads, toks = acts.shape
    wide = (hi - lo) // 2
    rows = heads // 16
    starts = [lo // wide if p.shape[1] > hi - lo else 0 for p in pieces]
    return pl.pallas_call(
        partial_kernel,
        grid_spec=pltpu.PrefetchScalarGridSpec(
            num_scalar_prefetch=1,
            grid=((hi - lo) // wide,),
            in_specs=[pl.BlockSpec(acts.shape, lambda i, at: (0, 0, 0, 0))]
            + [pl.BlockSpec((p.shape[0], wide), lambda i, at, s=s: (0, i + s)) for p, s in zip(pieces, starts)],
            out_specs=pl.BlockSpec((4, 4, rows, wide), lambda i, at: (0, 0, 0, i)),
            scratch_shapes=[pltpu.VMEM((heads, 8 * toks), BF16)],
        ),
        out_shape=jax.ShapeDtypeStruct((4, 4, rows, hi - lo), BF16),
        cost_estimate=pl.CostEstimate(
            flops=2 * heads * 8 * toks * (hi - lo), transcendentals=0,
            bytes_accessed=16 * toks * (hi - lo) + 2 * heads * (hi - lo) + 2 * acts.size),
        name="partial_grad_w",
    )(at, acts, *pieces)


def inputs_kernel(early, at, *refs):
    whole, pieces, weights, out, acc, lhs = refs[0], refs[1:11], refs[11:15], refs[15], refs[16], refs[17]
    y, l, c = at[1], at[2], at[3]
    k = pl.program_id(0)
    toks, heads = out.shape[3:]
    rhs = jnp.concatenate([w[...] for w in weights], axis=0)

    def product(tokens):
        return lax.dot_general(tokens, rhs, (((1,), (1,)), ((), ())), preferred_element_type=F32)

    @pl.when(k == 0)
    def _():
        acc[...] = product(whole[...])

    @pl.when((k > 0) & (k < early))
    def _():
        acc[...] += product(whole[...])

    @pl.when(k >= early)
    def _():
        for e in range(2):
            own, above, far_a, far_b, below = pieces[5 * e:5 * e + 5]
            for d, piece in ((0, own), (1, above), (3, below)):
                lhs[(y + d) & 3, (c + e) & 1] = piece[...]
            lhs[(y + 2) & 3, (c + e) & 1, :toks // 2] = far_a[...]
            lhs[(y + 2) & 3, (c + e) & 1, toks // 2:] = far_b[...]
        acc[...] += product(lhs[...].reshape(8 * toks, lhs.shape[3]))

    @pl.when(k == pl.num_programs(0) - 1)
    def _():
        for r in range(4):
            out[(l + r) & 3] = acc[:, r * heads:(r + 1) * heads].astype(out.dtype).reshape(4, 2, toks, heads)


def inputs_grad(at, whole, pieces, weights):
    heads, feats = weights[0].shape
    toks = pieces[0].shape[0]
    deep = feats // 8
    early = whole.shape[1] // deep
    late = [p.shape[1] // deep == 8 for p in pieces]
    return pl.pallas_call(
        lambda *refs: inputs_kernel(early, *refs),
        grid_spec=pltpu.PrefetchScalarGridSpec(
            num_scalar_prefetch=1,
            grid=(8,),
            in_specs=[pl.BlockSpec((8 * toks, deep), lambda k, at: (0, jnp.minimum(k, early - 1)))]
            + [pl.BlockSpec(
                (p.shape[0], deep), lambda k, at, s=early if full else 0: (0, jnp.maximum(k - early, 0) + s))
               for p, full in zip(pieces, late)]
            + [pl.BlockSpec((heads, deep), lambda k, at: (0, k)) for _ in weights],
            out_specs=pl.BlockSpec((4, 4, 2, toks, heads), lambda k, at: (0, 0, 0, 0, 0)),
            scratch_shapes=[pltpu.VMEM((8 * toks, 4 * heads), F32), pltpu.VMEM((4, 2, toks, deep), BF16)],
        ),
        out_shape=jax.ShapeDtypeStruct((4, 4, 2, toks, heads), BF16),
        cost_estimate=pl.CostEstimate(
            flops=2 * 8 * toks * feats * 4 * heads, transcendentals=0,
            bytes_accessed=2 * (8 * toks * feats + 4 * heads * feats + 32 * toks * heads)),
        name="grad_attn",
    )(at, whole, *pieces, *weights)


def local(grad_out, attn, w_out):
    g = grad_out[0]
    a = attn[0]
    toks, feats = g.shape
    heads = w_out.shape[0]
    at = jnp.stack([lax.axis_index(n) for n in ("x", "y", "l", "c")]).astype(jnp.int32)
    x, l = at[0], at[2]
    cut = SPLIT * feats // 8

    whole = lax.all_gather(g[:, :cut], ("y", "c"), axis=0, tiled=True)

    a = a.reshape(toks, 4, 4, 2, heads).transpose(1, 3, 2, 4, 0).reshape(8, 4 * heads, toks)
    acts = exchange(a, ("y", "c")).reshape(4, 2, 4 * heads, toks)

    w_above, w_below = shift(w_out, RING8, -1), shift(w_out, RING8, 1)

    half = toks // 2
    rest = g[:, cut:]
    above, below = shift(rest, "y", -1), shift(rest, "y", 1)

    acts = after(acts, w_above, w_below, above, below)
    part = partial(at, acts, [whole], 0, cut)
    w_far = shift(after(w_below, part), RING8, 1)
    weights = [w_out, w_above, w_far, w_below]
    tots = [lax.psum_scatter(part.reshape(16 * heads // 4, cut), "x", scatter_dimension=0, tiled=True)]

    pieces = [rest, above, shift(after(above[:half], part), "y", -1), shift(after(below[half:], part), "y", 1), below]
    pieces += [shift(p, "c", 1) for p in pieces]
    part = partial(at, after(acts, w_far), pieces, cut, feats)
    tots[0] = after(tots[0], part).reshape(4, heads // 4, cut)
    tots.append(exchange(part, "x"))

    res = inputs_grad(at, after(whole, part), pieces, weights)
    back = [pick(res, l)] + [shift(pick(res, (l + d) & 3), "l", d) for d in (1, 2, 3)]

    sums = []
    for j, tot in enumerate(tots):
        if j:
            tot = after(tot, acc).astype(F32).sum(0).astype(BF16)
        acc = pick(tot, l).astype(F32)
        for d in (1, -1, -2 if j % 2 else 2):
            acc = acc + shift(pick(tot, (l + d) & 3), RING8, d).astype(F32)
        acc = acc.astype(BF16)
        sums.append((acc.astype(F32) + shift(acc, "h", 1).astype(F32)).astype(BF16))
    acc = jnp.concatenate(sums, 1)
    grad_w = jnp.zeros((4, heads // 4, feats), BF16)
    for d in range(4):
        grad_w = lax.dynamic_update_slice_in_dim(
            grad_w, (shift(acc, "x", d) if d else acc)[None], (x - d) & 3, 0)
    grad_w = grad_w.reshape(heads, feats)

    out = jnp.zeros((4, 4, 2, toks, heads), BF16)
    for d, piece in enumerate(back):
        out = lax.dynamic_update_slice_in_dim(out, piece[:, None], (l - d) & 3, 1)
    out = out.reshape(1, 4 * 8 * toks, heads)
    return out, grad_w


def solution(mesh):
    fine = Mesh(mesh.devices.reshape(4, 2, 4, 4, 2), ("x", "h", "y", "l", "c"))
    dp, context = ("x", "h"), ("y", "l", "c")
    in_specs = (P(dp, context, None), P(dp, context, None), P(context, None))
    out_specs = (P(dp, None, context), P(context, None))
    return jax.shard_map(local, mesh=fine, in_specs=in_specs, out_specs=out_specs, check_vma=False)
```

```python
import jax
import jax.numpy as jnp
from jax import lax
from jax.experimental import pallas as pl
from jax.experimental.pallas import tpu as pltpu
from jax.sharding import Mesh, PartitionSpec as P

SPLIT = 4
RING8 = ("h", "l")
F32, BF16 = jnp.float32, jnp.bfloat16


def shift(v, axis, by):
    n = lax.axis_size(axis)
    return lax.ppermute(v, axis, [(i, (i + by) % n) for i in range(n)])


def exchange(v, axis):
    return lax.all_to_all(v, axis, split_axis=0, concat_axis=0, tiled=True)


def after(v, *others):
    return lax.optimization_barrier((v, *others))[0]


def pick(v, index):
    return lax.dynamic_index_in_dim(v, index, 0, keepdims=False)


def partial_kernel(lo, at, acts, *refs):
    pieces, (out, lhs, rhs, lhs_sems, rhs_sems) = refs[:10], refs[10:]
    y, c = at[1], at[3]
    blocks, _, wide = rhs.shape
    toks = acts.shape[3]

    def lhs_copy(k):
        e, d = divmod(k, 4)
        return pltpu.make_async_copy(
            acts.at[(y + d) & 3, (c + e) & 1], lhs.at[:, pl.ds(k * toks, toks)], lhs_sems.at[k])

    def rhs_copies(i):
        row = 0
        for k, piece in enumerate(pieces):
            yield pltpu.make_async_copy(
                piece.at[:, pl.ds(lo + i * wide, wide)], rhs.at[i, pl.ds(row, piece.shape[0])], rhs_sems.at[i, k])
            row += piece.shape[0]

    i = pl.program_id(0)

    @pl.when(i == 0)
    def _():
        for k in range(8):
            lhs_copy(k).start()
        for b in range(blocks):
            for copy in rhs_copies(b):
                copy.start()
        for k in range(8):
            lhs_copy(k).wait()

    for b in range(blocks):
        @pl.when(i == b)
        def _():
            for copy in rhs_copies(b):
                copy.wait()

    total = jnp.dot(lhs[...], rhs[i], preferred_element_type=F32).astype(out.dtype)
    parts, groups, rows, _ = out.shape
    for g in range(groups):
        for q in range(parts):
            r = (g * parts + q) * rows
            out[q, g] = total[r:r + rows]


def partial(at, acts, pieces, lo, hi):
    y, _, heads, toks = acts.shape
    wide = pieces[0].shape[1] // 8
    rows = heads // 16
    blocks = (hi - lo) // wide
    return pl.pallas_call(
        lambda *refs: partial_kernel(lo, *refs),
        grid_spec=pltpu.PrefetchScalarGridSpec(
            num_scalar_prefetch=1,
            grid=(blocks,),
            in_specs=[pl.BlockSpec(memory_space=pl.ANY)] * 11,
            out_specs=pl.BlockSpec((4, 4, rows, wide), lambda i, at: (0, 0, 0, i)),
            scratch_shapes=[
                pltpu.VMEM((heads, 8 * toks), BF16), pltpu.VMEM((blocks, 8 * toks, wide), BF16),
                pltpu.SemaphoreType.DMA((8,)), pltpu.SemaphoreType.DMA((blocks, 10))],
        ),
        out_shape=jax.ShapeDtypeStruct((4, 4, rows, hi - lo), BF16),
        cost_estimate=pl.CostEstimate(
            flops=2 * heads * 8 * toks * (hi - lo), transcendentals=0,
            bytes_accessed=16 * toks * (hi - lo) + 2 * heads * (hi - lo) + 2 * acts.size),
        name="partial_grad_w",
    )(at, acts, *pieces)


def inputs_kernel(at, *refs):
    pieces, weights, out, acc = refs[:10], refs[10:15], refs[15], refs[16]
    y, l, c = at[1], at[2], at[3]
    k = pl.program_id(0)
    lhs = jnp.concatenate([p[...] for p in pieces], axis=0)
    rhs = jnp.concatenate([w[...] for w in weights], axis=0)
    prod = lax.dot_general(lhs, rhs, (((1,), (1,)), ((), ())), preferred_element_type=F32)

    @pl.when(k == 0)
    def _():
        acc[...] = prod

    @pl.when(k > 0)
    def _():
        acc[...] += prod

    @pl.when(k == pl.num_programs(0) - 1)
    def _():
        toks, heads = out.shape[3:]
        for e in range(2):
            for d in range(4):
                t = (4 * e + d) * toks
                for r in range(4):
                    out[(l + r) & 3, (y + d) & 3, (c + e) & 1] = acc[
                        t:t + toks, r * heads:(r + 1) * heads].astype(out.dtype)


def inputs_grad(at, pieces, weights):
    heads, feats = weights[0].shape
    toks = pieces[0].shape[0]
    deep = feats // 4
    return pl.pallas_call(
        inputs_kernel,
        grid_spec=pltpu.PrefetchScalarGridSpec(
            num_scalar_prefetch=1,
            grid=(4,),
            in_specs=[pl.BlockSpec((p.shape[0], deep), lambda k, at: (0, k)) for p in (*pieces, *weights)],
            out_specs=pl.BlockSpec((4, 4, 2, toks, heads), lambda k, at: (0, 0, 0, 0, 0)),
            scratch_shapes=[pltpu.VMEM((8 * toks, 4 * heads), F32)],
        ),
        out_shape=jax.ShapeDtypeStruct((4, 4, 2, toks, heads), BF16),
        cost_estimate=pl.CostEstimate(
            flops=2 * 8 * toks * feats * 4 * heads, transcendentals=0,
            bytes_accessed=2 * (8 * toks * feats + 4 * heads * feats + 32 * toks * heads)),
        name="grad_attn",
    )(at, *pieces, *weights)


def local(grad_out, attn, w_out):
    g = grad_out[0]
    a = attn[0]
    toks, feats = g.shape
    heads = w_out.shape[0]
    at = jnp.stack([lax.axis_index(n) for n in ("x", "y", "l", "c")]).astype(jnp.int32)
    l = at[2]

    cut = SPLIT * feats // 8

    a = a.reshape(toks, 4, 4, 2, heads).transpose(1, 3, 2, 4, 0).reshape(8, 4 * heads, toks)
    acts = exchange(a, ("y", "c")).reshape(4, 2, 4 * heads, toks)

    half = toks // 2
    above, below = shift(g, "y", -1), shift(g, "y", 1)
    pieces = [g, above, shift(after(above[:half], acts), "y", -1), shift(after(below[half:], acts), "y", 1), below]
    pieces += [shift(p, "c", 1) for p in pieces]

    half = heads // 2
    w = after(w_out, a)
    w_above, w_below = shift(w, RING8, -1), shift(w, RING8, 1)
    w_far = [shift(w_above[:half], RING8, -1), shift(w_below[half:], RING8, 1)]

    part = partial(at, after(acts, *w_far), pieces, 0, cut)
    tot = lax.psum_scatter(part.reshape(4 * heads, cut), "x", scatter_dimension=0, tiled=True)
    part = partial(at, after(acts, part), pieces, cut, feats)
    other = exchange(part, "x")

    weights = [after(w_out, part), w_above, *w_far, w_below]
    res = inputs_grad(at, pieces, weights)
    back = [pick(res, l)] + [shift(pick(res, (l + d) & 3), "l", d) for d in (1, 2, 3)]

    other = after(other, *back[1:]).astype(F32).sum(0).astype(BF16)
    tot = jnp.concatenate([tot.reshape(4, heads // 4, cut), other], 2)
    x = at[0]
    half = heads // 8
    far = pick(tot, (l + 2) & 3)
    acc = pick(tot, l).astype(F32)
    for d in (1, -1):
        acc = acc + shift(pick(tot, (l + d) & 3), RING8, d).astype(F32)
    acc = acc + jnp.concatenate([shift(far[:half], RING8, -2), shift(far[half:], RING8, 2)], 0).astype(F32)
    acc = acc.astype(BF16)
    acc = (acc.astype(F32) + shift(acc, "h", 1).astype(F32)).astype(BF16)
    grad_w = jnp.zeros((4, heads // 4, feats), BF16)
    for d in range(4):
        grad_w = lax.dynamic_update_slice_in_dim(
            grad_w, (shift(acc, "x", d) if d else acc)[None], (x - d) & 3, 0)
    grad_w = grad_w.reshape(heads, feats)

    out = jnp.zeros((4, 4, 2, toks, heads), BF16)
    for d, piece in enumerate(back):
        out = lax.dynamic_update_slice_in_dim(out, piece[:, None], (l - d) & 3, 1)
    out = out.reshape(1, 4 * 8 * toks, heads)
    return out, grad_w


def solution(mesh):
    fine = Mesh(mesh.devices.reshape(4, 2, 4, 4, 2), ("x", "h", "y", "l", "c"))
    dp, context = ("x", "h"), ("y", "l", "c")
    in_specs = (P(dp, context, None), P(dp, context, None), P(context, None))
    out_specs = (P(dp, None, context), P(context, None))
    return jax.shard_map(local, mesh=fine, in_specs=in_specs, out_specs=out_specs, check_vma=False)
```

```python
import jax
import jax.numpy as jnp
from jax import lax
from jax.sharding import Mesh, PartitionSpec as P

RING8 = ("h", "l")
F32, BF16 = jnp.float32, jnp.bfloat16


def shift(v, axis, by):
    n = lax.axis_size(axis)
    return lax.ppermute(v, axis, [(i, (i + by) % n) for i in range(n)])


def exchange(v, axis):
    return lax.all_to_all(v, axis, split_axis=0, concat_axis=0, tiled=True)


def after(v, *others):
    return lax.optimization_barrier((v, *others))[0]


def pick(v, index, axis=0):
    return lax.dynamic_index_in_dim(v, index, axis, keepdims=False)


def put(buffer, piece, *at):
    at = at + (0,) * (buffer.ndim - len(at))
    return lax.dynamic_update_slice(buffer, piece.reshape((1,) * (buffer.ndim - piece.ndim) + piece.shape), at)


def add(a, b):
    return (a.astype(F32) + b.astype(F32)).astype(BF16)


def local(grad_out, attn, w_out):
    g = grad_out[0]
    a = attn[0]
    toks, feats = g.shape
    heads = w_out.shape[0]
    x, y, l, c = (lax.axis_index(n) for n in ("x", "y", "l", "c"))

    a = a.reshape(toks, 4, 4, 2, heads).transpose(1, 3, 0, 2, 4).reshape(8, toks, 4 * heads)
    acts = exchange(a, ("y", "c")).reshape(8 * toks, 4 * heads)

    half = toks // 2
    above, below = shift(g, "y", -1), shift(g, "y", 1)
    far_a, far_b = shift(after(above[:half], acts), "y", -1), shift(after(below[half:], acts), "y", 1)
    tokens = jnp.zeros((4, 2, toks, feats), BF16)
    for piece, d, row in ((g, 0, 0), (above, 1, 0), (below, 3, 0), (far_a, 2, 0), (far_b, 2, half)):
        tokens = put(tokens, piece, (y + d) & 3, c, row)
        tokens = put(tokens, shift(piece, "c", 1), (y + d) & 3, 1 - c, row)
    tokens = tokens.reshape(8 * toks, feats)

    half = heads // 2
    w = after(w_out, a)
    weights = put(jnp.zeros((4, heads, feats), BF16), w_out, l)
    for d in (1, -1):
        weights = put(weights, shift(w, RING8, -d), (l + d) & 3)
    weights = put(weights, shift(w[:half], RING8, 2), (l + 2) & 3, 0)
    weights = put(weights, shift(w[half:], RING8, -2), (l + 2) & 3, half)
    weights = weights.reshape(4 * heads, feats)

    part = lax.dot_general(acts, tokens, (((0,), (0,)), ((), ())), preferred_element_type=F32).astype(BF16)
    part = part.reshape(4, 4, heads // 4, feats)
    own, near_a, far, near_b = (pick(part, (x + d) & 3, 1) for d in range(4))
    half = heads // 8
    far_a, far_b = shift(far[:, :half], "x", 1), shift(far[:, half:], "x", -1)

    res = lax.dot_general(
        after(tokens, part), weights, (((1,), (1,)), ((), ())), preferred_element_type=F32).astype(BF16)
    res = res.reshape(4, 2, toks, 4, heads)
    back = [pick(res, l, 3)] + [shift(pick(res, (l + d) & 3, 3), "l", d) for d in (1, 2, 3)]

    far_a = after(far_a, res)
    near_a = jnp.concatenate([add(near_a[:, :half], far_a), near_a[:, half:]], 1)
    near_b = jnp.concatenate([near_b[:, :half], add(near_b[:, half:], far_b)], 1)
    tot = [own, shift(near_a, "x", 1), shift(near_b, "x", -1)]
    tot[0] = after(tot[0], *back[1:])
    tot = sum(t.astype(F32) for t in tot).astype(BF16)
    half = heads // 8
    far = pick(tot, (l + 2) & 3)
    acc = pick(tot, l).astype(F32)
    for d in (1, -1):
        acc = acc + shift(pick(tot, (l + d) & 3), RING8, d).astype(F32)
    acc = acc + jnp.concatenate([shift(far[:half], RING8, -2), shift(far[half:], RING8, 2)], 0).astype(F32)
    acc = acc.astype(BF16)
    acc = add(acc, shift(acc, "h", 1))
    grad_w = jnp.zeros((4, heads // 4, feats), BF16)
    for d in range(4):
        grad_w = put(grad_w, shift(acc, "x", d) if d else acc, (x - d) & 3)
    grad_w = grad_w.reshape(heads, feats)

    out = jnp.zeros((4, 4, 2, toks, heads), BF16)
    for d, piece in enumerate(back):
        out = lax.dynamic_update_slice_in_dim(out, piece[:, None], (l - d) & 3, 1)
    out = out.reshape(1, 4 * 8 * toks, heads)
    return out, grad_w


def solution(mesh):
    fine = Mesh(mesh.devices.reshape(4, 2, 4, 4, 2), ("x", "h", "y", "l", "c"))
    dp, context = ("x", "h"), ("y", "l", "c")
    in_specs = (P(dp, context, None), P(dp, context, None), P(context, None))
    out_specs = (P(dp, None, context), P(context, None))
    return jax.shard_map(local, mesh=fine, in_specs=in_specs, out_specs=out_specs, check_vma=False)
```

```python
import jax
import jax.numpy as jnp
from jax import lax
from jax.sharding import Mesh, PartitionSpec as P

RING8 = ("h", "l")
F32, BF16 = jnp.float32, jnp.bfloat16


def shift(v, axis, by):
    n = lax.axis_size(axis)
    return lax.ppermute(v, axis, [(i, (i + by) % n) for i in range(n)])


def exchange(v, axis):
    return lax.all_to_all(v, axis, split_axis=0, concat_axis=0, tiled=True)


def after(v, *others):
    return lax.optimization_barrier((v, *others))[0]


def pick(v, index, axis=0):
    return lax.dynamic_index_in_dim(v, index, axis, keepdims=False)


def put(buffer, piece, *at):
    at = at + (0,) * (buffer.ndim - len(at))
    return lax.dynamic_update_slice(buffer, piece.reshape((1,) * (buffer.ndim - piece.ndim) + piece.shape), at)


def add(a, b):
    return (a.astype(F32) + b.astype(F32)).astype(BF16)


def local(grad_out, attn, w_out):
    g = grad_out[0]
    a = attn[0]
    toks, feats = g.shape
    heads = w_out.shape[0]
    x, y, l, c = (lax.axis_index(n) for n in ("x", "y", "l", "c"))

    a = a.reshape(toks, 4, 4, 2, heads).transpose(1, 3, 0, 2, 4).reshape(8, toks, 4 * heads)
    acts = exchange(a, ("y", "c")).reshape(8 * toks, 4 * heads)

    half = toks // 2
    above, below = shift(g, "y", -1), shift(g, "y", 1)
    far_a, far_b = shift(after(above[:half], acts), "y", -1), shift(after(below[half:], acts), "y", 1)
    tokens = jnp.zeros((4, 2, toks, feats), BF16)
    for piece, d, row in ((g, 0, 0), (above, 1, 0), (below, 3, 0), (far_a, 2, 0), (far_b, 2, half)):
        tokens = put(tokens, piece, (y + d) & 3, c, row)
        tokens = put(tokens, shift(piece, "c", 1), (y + d) & 3, 1 - c, row)
    tokens = tokens.reshape(8 * toks, feats)

    def partial(r, source):
        columns = lax.dynamic_slice_in_dim(source, ((x + r) & 3) * cols, cols, 1)
        return lax.dot_general(columns, acts, (((0,), (0,)), ((), ())), preferred_element_type=F32).astype(BF16)

    cols = feats // 4
    far = partial(2, tokens)
    top, bottom = shift(far[:cols // 2], "x", 1), shift(far[cols // 2:], "x", -1)

    half = heads // 2
    w = after(w_out, a)
    w_above, w_below = shift(w, RING8, -1), shift(w, RING8, 1)
    weights = jnp.zeros((4, heads, feats), BF16)
    for piece, d in ((w_out, 0), (w_above, 1), (w_below, 3)):
        weights = put(weights, piece, (l + d) & 3)
    w_far_a = shift(after(w_above[:half], far_a), RING8, -1)
    w_far_b = shift(after(w_below[half:], far_a), RING8, 1)
    weights = put(weights, after(w_far_a, top), (l + 2) & 3, 0)
    weights = put(weights, after(w_far_b, top), (l + 2) & 3, half)
    weights = weights.reshape(4 * heads, feats)

    res = lax.dot_general(
        after(tokens, far), weights, (((1,), (1,)), ((), ())), preferred_element_type=F32).astype(BF16)

    def block(v, k):
        return lax.dynamic_slice_in_dim(v, (k & 3) * heads, heads, 1)

    back = [block(res, l)] + [shift(block(res, l + d), "l", d) for d in (1, 2, 3)]

    near_a, near_b = partial(1, after(tokens, top)), partial(3, after(tokens, bottom))
    near_a = lax.dynamic_update_slice(near_a, add(near_a[:cols // 2], top), (0, 0))
    near_b = lax.dynamic_update_slice(near_b, add(near_b[cols // 2:], bottom), (cols // 2, 0))
    own = partial(0, after(tokens, near_b))
    tot = [after(own, *back[1:]), shift(near_a, "x", 1), shift(near_b, "x", -1)]
    tot = sum(t.astype(F32) for t in tot).astype(BF16)
    far = block(tot, l + 2)
    acc = block(tot, l).astype(F32)
    for d in (1, -1):
        acc = acc + shift(block(tot, l + d), RING8, d).astype(F32)
    acc = acc + jnp.concatenate(
        [shift(far[:cols // 2], RING8, -2), shift(far[cols // 2:], RING8, 2)], 0).astype(F32)
    acc = acc.astype(BF16)
    acc = add(acc, shift(acc, "h", 1)).T
    grad_w = jnp.zeros((heads, feats), BF16)
    for d in range(4):
        grad_w = lax.dynamic_update_slice(
            grad_w, shift(acc, "x", d) if d else acc, (0, ((x - d) & 3) * cols))

    out = jnp.zeros((4, 4, 2 * toks, heads), BF16)
    for d, piece in enumerate(back):
        out = lax.dynamic_update_slice_in_dim(out, piece.reshape(4, 1, 2 * toks, heads), (l - d) & 3, 1)
    out = out.reshape(1, 4 * 8 * toks, heads)
    return out, grad_w


def solution(mesh):
    fine = Mesh(mesh.devices.reshape(4, 2, 4, 4, 2), ("x", "h", "y", "l", "c"))
    dp, context = ("x", "h"), ("y", "l", "c")
    in_specs = (P(dp, context, None), P(dp, context, None), P(context, None))
    out_specs = (P(dp, None, context), P(context, None))
    return jax.shard_map(local, mesh=fine, in_specs=in_specs, out_specs=out_specs, check_vma=False)
```

```python
import jax
import jax.numpy as jnp
from jax import lax
from jax.sharding import Mesh, PartitionSpec as P

RING8 = ("h", "l")
F32, BF16 = jnp.float32, jnp.bfloat16


def shift(v, axis, by):
    n = lax.axis_size(axis)
    return lax.ppermute(v, axis, [(i, (i + by) % n) for i in range(n)])


def exchange(v, axis):
    return lax.all_to_all(v, axis, split_axis=0, concat_axis=0, tiled=True)


def after(v, *others):
    return lax.optimization_barrier((v, *others))[0]


def pick(v, index, axis=0):
    return lax.dynamic_index_in_dim(v, index, axis, keepdims=False)


def put(buffer, piece, *at):
    at = at + (0,) * (buffer.ndim - len(at))
    return lax.dynamic_update_slice(buffer, piece.reshape((1,) * (buffer.ndim - piece.ndim) + piece.shape), at)


def add(a, b):
    return (a.astype(F32) + b.astype(F32)).astype(BF16)


def local(grad_out, attn, w_out):
    g = grad_out[0]
    a = attn[0]
    toks, feats = g.shape
    heads = w_out.shape[0]
    x, y, l, c = (lax.axis_index(n) for n in ("x", "y", "l", "c"))

    a = a.reshape(toks, 4, 4, 2, heads).transpose(1, 3, 0, 2, 4).reshape(8, toks, 4 * heads)
    acts = exchange(a, ("y", "c")).reshape(8 * toks, 4 * heads)

    half = toks // 2
    above, below = shift(g, "y", -1), shift(g, "y", 1)
    far_a, far_b = shift(after(above[:half], acts), "y", -1), shift(after(below[half:], acts), "y", 1)
    tokens = jnp.zeros((4, 2, toks, feats), BF16)
    for piece, d, row in ((g, 0, 0), (above, 1, 0), (below, 3, 0), (far_a, 2, 0), (far_b, 2, half)):
        tokens = put(tokens, piece, (y + d) & 3, c, row)
        tokens = put(tokens, shift(piece, "c", 1), (y + d) & 3, 1 - c, row)
    tokens = tokens.reshape(8 * toks, feats)

    def partial(r, source):
        columns = lax.dynamic_slice_in_dim(source, ((x + r) & 3) * cols, cols, 1)
        return lax.dot_general(columns, acts, (((0,), (0,)), ((), ())), preferred_element_type=F32).astype(BF16)

    cols = feats // 4
    far = partial(2, tokens)
    top, bottom = shift(far[:cols // 2], "x", 1), shift(far[cols // 2:], "x", -1)

    half = heads // 2
    w = after(w_out, a)
    w_above, w_below = shift(w, RING8, -1), shift(w, RING8, 1)
    weights = jnp.zeros((4, heads, feats), BF16)
    for piece, d in ((w_out, 0), (w_above, 1), (w_below, 3)):
        weights = put(weights, piece, (l + d) & 3)
    w_far_a = shift(after(w_above[:half], far_a), RING8, -1)
    w_far_b = shift(after(w_below[half:], far_a), RING8, 1)
    weights = put(weights, after(w_far_a, far), (l + 2) & 3, 0)
    weights = put(weights, after(w_far_b, far), (l + 2) & 3, half)
    weights = weights.reshape(4 * heads, feats)

    res = lax.dot_general(
        after(tokens, far), weights, (((1,), (1,)), ((), ())), preferred_element_type=F32).astype(BF16)

    def block(v, k):
        return lax.dynamic_slice_in_dim(v, (k & 3) * heads, heads, 1)

    back = [block(res, l)] + [shift(block(res, l + d), "l", d) for d in (1, 2, 3)]

    near_a, near_b = partial(1, after(tokens, top, res)), partial(3, after(tokens, bottom, res))
    near_a = lax.dynamic_update_slice(near_a, add(near_a[:cols // 2], top), (0, 0))
    near_b = lax.dynamic_update_slice(near_b, add(near_b[cols // 2:], bottom), (cols // 2, 0))
    own = partial(0, after(tokens, near_b))
    tot = [after(own, *back[1:]), shift(near_a, "x", 1), shift(near_b, "x", -1)]
    tot = sum(t.astype(F32) for t in tot).astype(BF16)
    far = block(tot, l + 2)
    acc = block(tot, l).astype(F32)
    for d in (1, -1):
        acc = acc + shift(block(tot, l + d), RING8, d).astype(F32)
    acc = acc + jnp.concatenate(
        [shift(far[:cols // 2], RING8, -2), shift(far[cols // 2:], RING8, 2)], 0).astype(F32)
    acc = acc.astype(BF16)
    acc = add(acc, shift(acc, "h", 1)).T
    grad_w = jnp.zeros((heads, feats), BF16)
    for d in range(4):
        grad_w = lax.dynamic_update_slice(
            grad_w, shift(acc, "x", d) if d else acc, (0, ((x - d) & 3) * cols))

    out = jnp.zeros((4, 4, 2 * toks, heads), BF16)
    for d, piece in enumerate(back):
        out = lax.dynamic_update_slice_in_dim(out, piece.reshape(4, 1, 2 * toks, heads), (l - d) & 3, 1)
    out = out.reshape(1, 4 * 8 * toks, heads)
    return out, grad_w


def solution(mesh):
    fine = Mesh(mesh.devices.reshape(4, 2, 4, 4, 2), ("x", "h", "y", "l", "c"))
    dp, context = ("x", "h"), ("y", "l", "c")
    in_specs = (P(dp, context, None), P(dp, context, None), P(context, None))
    out_specs = (P(dp, None, context), P(context, None))
    return jax.shard_map(local, mesh=fine, in_specs=in_specs, out_specs=out_specs, check_vma=False)
```

```python
import jax
import jax.numpy as jnp
from jax import lax
from jax.sharding import Mesh, PartitionSpec as P

RING8 = ("h", "l")
F32, BF16 = jnp.float32, jnp.bfloat16


def shift(v, axis, by):
    n = lax.axis_size(axis)
    return lax.ppermute(v, axis, [(i, (i + by) % n) for i in range(n)])


def exchange(v, axis):
    return lax.all_to_all(v, axis, split_axis=0, concat_axis=0, tiled=True)


def after(v, *others):
    return lax.optimization_barrier((v, *others))[0]


def pick(v, index, axis=0):
    return lax.dynamic_index_in_dim(v, index, axis, keepdims=False)


def put(buffer, piece, *at):
    at = at + (0,) * (buffer.ndim - len(at))
    return lax.dynamic_update_slice(buffer, piece.reshape((1,) * (buffer.ndim - piece.ndim) + piece.shape), at)


def add(a, b):
    return (a.astype(F32) + b.astype(F32)).astype(BF16)


def local(grad_out, attn, w_out):
    g = grad_out[0]
    a = attn[0]
    toks, feats = g.shape
    heads = w_out.shape[0]
    x, y, l, c = (lax.axis_index(n) for n in ("x", "y", "l", "c"))

    a = a.reshape(toks, 4, 4, 2, heads).transpose(1, 3, 0, 2, 4).reshape(8, toks, 4 * heads)
    acts = exchange(a, ("y", "c")).reshape(8 * toks, 4 * heads)

    half = toks // 2
    above, below = shift(g, "y", -1), shift(g, "y", 1)
    far_a, far_b = shift(after(above[:half], acts), "y", -1), shift(after(below[half:], acts), "y", 1)
    tokens = jnp.zeros((4, 2, toks, feats), BF16)
    for piece, d, row in ((g, 0, 0), (above, 1, 0), (below, 3, 0), (far_a, 2, 0), (far_b, 2, half)):
        tokens = put(tokens, piece, (y + d) & 3, c, row)
        tokens = put(tokens, shift(piece, "c", 1), (y + d) & 3, 1 - c, row)
    tokens = tokens.reshape(8 * toks, feats)

    def partial(r, source, more=0.0):
        columns = lax.dynamic_slice_in_dim(source, ((x + r) & 3) * cols, cols, 1)
        total = lax.dot_general(columns, acts, (((0,), (0,)), ((), ())), preferred_element_type=F32)
        return (total + more).astype(BF16)

    cols = feats // 4
    far = partial(2, tokens)
    top, bottom = shift(far[:cols // 2], "x", 1), shift(far[cols // 2:], "x", -1)

    half = heads // 2
    w = after(w_out, a)
    w_above, w_below = shift(w, RING8, -1), shift(w, RING8, 1)
    weights = jnp.zeros((4, heads, feats), BF16)
    for piece, d in ((w_out, 0), (w_above, 1), (w_below, 3)):
        weights = put(weights, piece, (l + d) & 3)
    w_far_a = shift(after(w_above[:half], far_a), RING8, -1)
    w_far_b = shift(after(w_below[half:], far_a), RING8, 1)
    weights = put(weights, after(w_far_a, far), (l + 2) & 3, 0)
    weights = put(weights, after(w_far_b, far), (l + 2) & 3, half)
    weights = weights.reshape(4 * heads, feats)

    res = lax.dot_general(
        after(tokens, far), weights, (((1,), (1,)), ((), ())), preferred_element_type=F32).astype(BF16)

    def block(v, k):
        return lax.dynamic_slice_in_dim(v, (k & 3) * heads, heads, 1)

    back = [block(res, l)] + [shift(block(res, l + d), "l", d) for d in (1, 2, 3)]

    none = jnp.zeros((), BF16)
    top = lax.pad(top, none, ((0, cols // 2, 0), (0, 0, 0))).astype(F32)
    bottom = lax.pad(bottom, none, ((cols // 2, 0, 0), (0, 0, 0))).astype(F32)
    near_a, near_b = partial(1, after(tokens, res), top), partial(3, after(tokens, res), bottom)
    own = partial(0, after(tokens, near_b))
    tot = [after(own, *back[1:]), shift(near_a, "x", 1), shift(near_b, "x", -1)]
    tot = sum(t.astype(F32) for t in tot).astype(BF16)
    far = block(tot, l + 2)
    acc = block(tot, l).astype(F32)
    for d in (1, -1):
        acc = acc + shift(block(tot, l + d), RING8, d).astype(F32)
    acc = acc + jnp.concatenate(
        [shift(far[:cols // 2], RING8, -2), shift(far[cols // 2:], RING8, 2)], 0).astype(F32)
    acc = acc.astype(BF16)
    acc = add(acc, shift(acc, "h", 1)).T
    grad_w = jnp.zeros((heads, feats), BF16)
    for d in range(4):
        grad_w = lax.dynamic_update_slice(
            grad_w, shift(acc, "x", d) if d else acc, (0, ((x - d) & 3) * cols))

    out = jnp.zeros((4, 4, 2 * toks, heads), BF16)
    for d, piece in enumerate(back):
        out = lax.dynamic_update_slice_in_dim(out, piece.reshape(4, 1, 2 * toks, heads), (l - d) & 3, 1)
    out = out.reshape(1, 4 * 8 * toks, heads)
    return out, grad_w


def solution(mesh):
    fine = Mesh(mesh.devices.reshape(4, 2, 4, 4, 2), ("x", "h", "y", "l", "c"))
    dp, context = ("x", "h"), ("y", "l", "c")
    in_specs = (P(dp, context, None), P(dp, context, None), P(context, None))
    out_specs = (P(dp, None, context), P(context, None))
    return jax.shard_map(local, mesh=fine, in_specs=in_specs, out_specs=out_specs, check_vma=False)
```

```python
import jax
import jax.numpy as jnp
from jax import lax
from jax.sharding import Mesh, PartitionSpec as P

RING8 = ("h", "l")
F32, BF16 = jnp.float32, jnp.bfloat16


def shift(v, axis, by):
    n = lax.axis_size(axis)
    return lax.ppermute(v, axis, [(i, (i + by) % n) for i in range(n)])


def exchange(v, axis):
    return lax.all_to_all(v, axis, split_axis=0, concat_axis=0, tiled=True)


def after(v, *others):
    return lax.optimization_barrier((v, *others))[0]


def pick(v, index, axis=0):
    return lax.dynamic_index_in_dim(v, index, axis, keepdims=False)


def put(buffer, piece, *at):
    at = at + (0,) * (buffer.ndim - len(at))
    return lax.dynamic_update_slice(buffer, piece.reshape((1,) * (buffer.ndim - piece.ndim) + piece.shape), at)


def add(a, b):
    return (a.astype(F32) + b.astype(F32)).astype(BF16)


def local(grad_out, attn, w_out):
    g = grad_out[0]
    a = attn[0]
    toks, feats = g.shape
    heads = w_out.shape[0]
    x, y, l, c = (lax.axis_index(n) for n in ("x", "y", "l", "c"))

    a = a.reshape(toks, 4, 4, 2, heads).transpose(1, 3, 0, 2, 4).reshape(8, toks, 4 * heads)
    acts = exchange(a, ("y", "c")).reshape(8 * toks, 4 * heads)

    half = toks // 2
    above, below = shift(g, "y", -1), shift(g, "y", 1)
    half_a, half_b = after(above[:half], acts), after(below[half:], acts)
    far_a, far_b = shift(half_a, "y", -1), shift(half_b, "y", 1)
    tokens = jnp.zeros((4, 2, toks, feats), BF16)
    for piece, d in ((g, 0), (above, 1), (below, 3), (jnp.concatenate([far_a, far_b]), 2)):
        tokens = put(tokens, piece, (y + d) & 3, c)
        tokens = put(tokens, shift(piece, "c", 1), (y + d) & 3, 1 - c)
    tokens = tokens.reshape(8 * toks, feats)

    def partial(r, source, more=0.0):
        columns = lax.dynamic_slice_in_dim(source, ((x + r) & 3) * cols, cols, 1)
        total = lax.dot_general(columns, acts, (((0,), (0,)), ((), ())), preferred_element_type=F32)
        return (total + more).astype(BF16)

    cols = feats // 4
    far = partial(2, tokens)
    top, bottom = shift(far[:cols // 2], "x", 1), shift(far[cols // 2:], "x", -1)

    half = heads // 2
    w = after(w_out, a)
    w_above, w_below = shift(w, RING8, -1), shift(w, RING8, 1)
    weights = jnp.zeros((4, heads, feats), BF16)
    for piece, d in ((w_out, 0), (w_above, 1), (w_below, 3)):
        weights = put(weights, piece, (l + d) & 3)
    w_far_a = shift(after(w_above[:half], half_a, half_b), RING8, -1)
    w_far_b = shift(after(w_below[half:], half_a, half_b), RING8, 1)
    weights = put(weights, after(w_far_a, far), (l + 2) & 3, 0)
    weights = put(weights, after(w_far_b, far), (l + 2) & 3, half)
    weights = weights.reshape(4 * heads, feats)

    res = lax.dot_general(
        after(tokens, far), weights, (((1,), (1,)), ((), ())), preferred_element_type=F32).astype(BF16)

    def block(v, k):
        return lax.dynamic_slice_in_dim(v, (k & 3) * heads, heads, 1)

    back = [block(res, l)] + [shift(block(res, l + d), "l", d) for d in (1, 2, 3)]

    none = jnp.zeros((), BF16)
    top = lax.pad(top, none, ((0, cols // 2, 0), (0, 0, 0))).astype(F32)
    bottom = lax.pad(bottom, none, ((cols // 2, 0, 0), (0, 0, 0))).astype(F32)
    near_a, near_b = partial(1, after(tokens, res), top), partial(3, after(tokens, res), bottom)
    own = partial(0, after(tokens, near_b))
    tot = [after(own, *back[1:]), shift(near_a, "x", 1), shift(near_b, "x", -1)]
    tot = sum(t.astype(F32) for t in tot).astype(BF16)
    far = block(tot, l + 2)
    acc = block(tot, l).astype(F32)
    for d in (1, -1):
        acc = acc + shift(block(tot, l + d), RING8, d).astype(F32)
    acc = acc + jnp.concatenate(
        [shift(far[:cols // 2], RING8, -2), shift(far[cols // 2:], RING8, 2)], 0).astype(F32)
    acc = acc.astype(BF16)
    acc = add(acc, shift(acc, "h", 1)).T
    grad_w = jnp.zeros((heads, feats), BF16)
    for d in range(4):
        grad_w = lax.dynamic_update_slice(
            grad_w, shift(acc, "x", d) if d else acc, (0, ((x - d) & 3) * cols))

    out = jnp.zeros((4, 4, 2 * toks, heads), BF16)
    for d, piece in enumerate(back):
        out = lax.dynamic_update_slice_in_dim(out, piece.reshape(4, 1, 2 * toks, heads), (l - d) & 3, 1)
    out = out.reshape(1, 4 * 8 * toks, heads)
    return out, grad_w


def solution(mesh):
    fine = Mesh(mesh.devices.reshape(4, 2, 4, 4, 2), ("x", "h", "y", "l", "c"))
    dp, context = ("x", "h"), ("y", "l", "c")
    in_specs = (P(dp, context, None), P(dp, context, None), P(context, None))
    out_specs = (P(dp, None, context), P(context, None))
    return jax.shard_map(local, mesh=fine, in_specs=in_specs, out_specs=out_specs, check_vma=False)
```

```python
import jax
import jax.numpy as jnp
from jax import lax
from jax.sharding import Mesh, PartitionSpec as P

RING8 = ("h", "l")
F32, BF16 = jnp.float32, jnp.bfloat16


def shift(v, axis, by):
    n = lax.axis_size(axis)
    return lax.ppermute(v, axis, [(i, (i + by) % n) for i in range(n)])


def exchange(v, axis):
    return lax.all_to_all(v, axis, split_axis=0, concat_axis=0, tiled=True)


def after(v, *others):
    return lax.optimization_barrier((v, *others))[0]


def pick(v, index, axis=0):
    return lax.dynamic_index_in_dim(v, index, axis, keepdims=False)


def put(buffer, piece, *at):
    at = at + (0,) * (buffer.ndim - len(at))
    return lax.dynamic_update_slice(buffer, piece.reshape((1,) * (buffer.ndim - piece.ndim) + piece.shape), at)


def add(a, b):
    return (a.astype(F32) + b.astype(F32)).astype(BF16)


def local(grad_out, attn, w_out):
    g = grad_out[0]
    a = attn[0]
    toks, feats = g.shape
    heads = w_out.shape[0]
    x, y, l, c = (lax.axis_index(n) for n in ("x", "y", "l", "c"))

    a = a.reshape(toks, 4, 4, 2, heads).transpose(1, 3, 0, 2, 4).reshape(8, toks, 4 * heads)
    acts = exchange(a, ("y", "c")).reshape(8 * toks, 4 * heads)

    half = toks // 2
    above, below = shift(g, "y", -1), shift(g, "y", 1)
    half_a, half_b = after(above[:half], acts), after(below[half:], acts)
    far_a, far_b = shift(half_a, "y", -1), shift(half_b, "y", 1)
    tokens = jnp.zeros((4, 2, toks, feats), BF16)
    for piece, d in ((g, 0), (above, 1), (below, 3), (jnp.concatenate([far_a, far_b]), 2)):
        tokens = put(tokens, piece, (y + d) & 3, c)
        tokens = put(tokens, shift(piece, "c", 1), (y + d) & 3, 1 - c)
    tokens = tokens.reshape(8 * toks, feats)

    def partial(r, source, more=0.0):
        columns = lax.dynamic_slice_in_dim(source, ((x + r) & 3) * cols, cols, 1)
        total = lax.dot_general(columns, acts, (((0,), (0,)), ((), ())), preferred_element_type=F32)
        return (total + more).astype(BF16)

    cols = feats // 4
    far = partial(2, tokens)
    top, bottom = shift(far[:cols // 2], "x", 1), shift(far[cols // 2:], "x", -1)

    half = heads // 2
    w = after(w_out, a)
    w_above, w_below = shift(w, RING8, -1), shift(w, RING8, 1)
    weights = jnp.zeros((4, heads, feats), BF16)
    weights = put(weights, w_out, l)
    for piece, d in ((w_above, 1), (w_below, 3)):
        weights = put(weights, after(piece, far), (l + d) & 3)
    w_far_a = shift(after(w_above[:half], half_a, half_b), RING8, -1)
    w_far_b = shift(after(w_below[half:], half_a, half_b), RING8, 1)
    weights = put(weights, after(w_far_a, far), (l + 2) & 3, 0)
    weights = put(weights, after(w_far_b, far), (l + 2) & 3, half)
    weights = weights.reshape(4 * heads, feats)

    res = lax.dot_general(
        after(tokens, far), weights, (((1,), (1,)), ((), ())), preferred_element_type=F32).astype(BF16)

    def block(v, k):
        return lax.dynamic_slice_in_dim(v, (k & 3) * heads, heads, 1)

    back = [block(res, l)] + [shift(block(res, l + d), "l", d) for d in (1, 2, 3)]

    none = jnp.zeros((), BF16)
    top = lax.pad(top, none, ((0, cols // 2, 0), (0, 0, 0))).astype(F32)
    bottom = lax.pad(bottom, none, ((cols // 2, 0, 0), (0, 0, 0))).astype(F32)
    near_a, near_b = partial(1, after(tokens, res), top), partial(3, after(tokens, res), bottom)
    own = partial(0, after(tokens, near_b))
    tot = [after(own, *back[1:]), shift(near_a, "x", 1), shift(near_b, "x", -1)]
    tot = sum(t.astype(F32) for t in tot).astype(BF16)
    far = block(tot, l + 2)
    acc = block(tot, l).astype(F32)
    for d in (1, -1):
        acc = acc + shift(block(tot, l + d), RING8, d).astype(F32)
    acc = acc + jnp.concatenate(
        [shift(far[:cols // 2], RING8, -2), shift(far[cols // 2:], RING8, 2)], 0).astype(F32)
    acc = acc.astype(BF16)
    acc = add(acc, shift(acc, "h", 1)).T
    grad_w = jnp.zeros((heads, feats), BF16)
    for d in range(4):
        grad_w = lax.dynamic_update_slice(
            grad_w, shift(acc, "x", d) if d else acc, (0, ((x - d) & 3) * cols))

    out = jnp.zeros((4, 4, 2 * toks, heads), BF16)
    for d, piece in enumerate(back):
        out = lax.dynamic_update_slice_in_dim(out, piece.reshape(4, 1, 2 * toks, heads), (l - d) & 3, 1)
    out = out.reshape(1, 4 * 8 * toks, heads)
    return out, grad_w


def solution(mesh):
    fine = Mesh(mesh.devices.reshape(4, 2, 4, 4, 2), ("x", "h", "y", "l", "c"))
    dp, context = ("x", "h"), ("y", "l", "c")
    in_specs = (P(dp, context, None), P(dp, context, None), P(context, None))
    out_specs = (P(dp, None, context), P(context, None))
    return jax.shard_map(local, mesh=fine, in_specs=in_specs, out_specs=out_specs, check_vma=False)
```

```python
import jax
import jax.numpy as jnp
from jax import lax
from jax.sharding import Mesh, PartitionSpec as P

RING8 = ("h", "l")
F32, BF16 = jnp.float32, jnp.bfloat16


def shift(v, axis, by):
    n = lax.axis_size(axis)
    return lax.ppermute(v, axis, [(i, (i + by) % n) for i in range(n)])


def exchange(v, axis):
    return lax.all_to_all(v, axis, split_axis=0, concat_axis=0, tiled=True)


def after(v, *others):
    return lax.optimization_barrier((v, *others))[0]


def pick(v, index, axis=0):
    return lax.dynamic_index_in_dim(v, index, axis, keepdims=False)


def put(buffer, piece, *at):
    at = at + (0,) * (buffer.ndim - len(at))
    return lax.dynamic_update_slice(buffer, piece.reshape((1,) * (buffer.ndim - piece.ndim) + piece.shape), at)


def add(a, b):
    return (a.astype(F32) + b.astype(F32)).astype(BF16)


def local(grad_out, attn, w_out):
    g = grad_out[0]
    a = attn[0]
    toks, feats = g.shape
    heads = w_out.shape[0]
    x, y, l, c = (lax.axis_index(n) for n in ("x", "y", "l", "c"))

    a = a.reshape(toks, 4, 4, 2, heads).transpose(1, 3, 0, 2, 4).reshape(8, toks, 4 * heads)
    acts = exchange(a, ("y", "c")).reshape(8 * toks, 4 * heads)

    half = toks // 2
    above, below = shift(g, "y", -1), shift(g, "y", 1)
    half_a, half_b = after(above[:half], acts), after(below[half:], acts)
    far_a, far_b = shift(half_a, "y", -1), shift(half_b, "y", 1)
    tokens = jnp.zeros((4, 2, toks, feats), BF16)
    for piece, d in ((g, 0), (above, 1), (below, 3), (jnp.concatenate([far_a, far_b]), 2)):
        tokens = put(tokens, piece, (y + d) & 3, c)
        tokens = put(tokens, shift(piece, "c", 1), (y + d) & 3, 1 - c)
    tokens = tokens.reshape(8 * toks, feats)

    def partial(r, source, more=0.0):
        columns = lax.dynamic_slice_in_dim(source, ((x + r) & 3) * cols, cols, 1)
        total = lax.dot_general(columns, acts, (((0,), (0,)), ((), ())), preferred_element_type=F32)
        return (total + more).astype(BF16)

    cols = feats // 4
    far = partial(2, tokens)
    top, bottom = shift(far[:cols // 2], "x", 1), shift(far[cols // 2:], "x", -1)

    half = heads // 2
    w = after(w_out, a)
    w_above, w_below = shift(w, RING8, -1), shift(w, RING8, 1)
    weights = jnp.zeros((4, heads, feats), BF16)
    for piece, d in ((w_out, 0), (w_above, 1), (w_below, 3)):
        weights = put(weights, piece, (l + d) & 3)
    w_far_a = shift(after(w_above[:half], half_a, half_b), RING8, -1)
    w_far_b = shift(after(w_below[half:], half_a, half_b), RING8, 1)
    weights = put(weights, after(w_far_a, far), (l + 2) & 3, 0)
    weights = put(weights, after(w_far_b, far), (l + 2) & 3, half)
    weights = weights.reshape(4 * heads, feats)

    res = lax.dot_general(
        after(tokens, far), weights, (((1,), (1,)), ((), ())), preferred_element_type=F32).astype(BF16)

    def block(v, k):
        return lax.dynamic_slice_in_dim(v, (k & 3) * heads, heads, 1)

    back = [block(res, l)] + [shift(block(res, l + d), "l", d) for d in (1, 2, 3)]

    none = jnp.zeros((), BF16)
    top = lax.pad(top, none, ((0, cols // 2, 0), (0, 0, 0))).astype(F32)
    bottom = lax.pad(bottom, none, ((cols // 2, 0, 0), (0, 0, 0))).astype(F32)
    near_a, near_b = partial(1, after(tokens, res), top), partial(3, after(tokens, res), bottom)
    own = partial(0, after(tokens, near_b))
    tot = [own, shift(near_a, "x", 1), shift(near_b, "x", -1)]
    tot = sum(t.astype(F32) for t in tot).astype(BF16)
    far = block(tot, l + 2)
    acc = block(tot, l).astype(F32)
    for d in (1, -1):
        acc = acc + shift(block(tot, l + d), RING8, d).astype(F32)
    acc = acc + jnp.concatenate(
        [shift(far[:cols // 2], RING8, -2), shift(far[cols // 2:], RING8, 2)], 0).astype(F32)
    acc = acc.astype(BF16)
    acc = add(acc, shift(acc, "h", 1)).T
    grad_w = jnp.zeros((heads, feats), BF16)
    for d in range(4):
        grad_w = lax.dynamic_update_slice(
            grad_w, shift(acc, "x", d) if d else acc, (0, ((x - d) & 3) * cols))

    out = jnp.zeros((4, 4, 2 * toks, heads), BF16)
    for d, piece in enumerate(back):
        out = lax.dynamic_update_slice_in_dim(out, piece.reshape(4, 1, 2 * toks, heads), (l - d) & 3, 1)
    out = out.reshape(1, 4 * 8 * toks, heads)
    return out, grad_w


def solution(mesh):
    fine = Mesh(mesh.devices.reshape(4, 2, 4, 4, 2), ("x", "h", "y", "l", "c"))
    dp, context = ("x", "h"), ("y", "l", "c")
    in_specs = (P(dp, context, None), P(dp, context, None), P(context, None))
    out_specs = (P(dp, None, context), P(context, None))
    return jax.shard_map(local, mesh=fine, in_specs=in_specs, out_specs=out_specs, check_vma=False)
```
